256 devices in a mesh: layer: 8 (over y, z_lo), dp: 32 (over x, z_hi, core).
Axes of the slice: x: 4, y: 4, z: 8 (z_hi: 4, z_lo: 2; z = z_hi * 2 + z_lo), core: 2. Of those that a mesh axis runs over, the one named last changes fastest.
Arguments:
- states: bfloat16 [24, 64, 32, 32, 128], P('layer', 'dp'), may hold values from -6 to 6
- weights: bfloat16 [24, 1152, 128], P('layer'), may hold values from -0.1875 to 0.1875
- bias: float32 [24, 128], P('layer'), may hold values from -3 to 3
- guesses: float32 [8, 64, 32, 32, 128], P('layer', 'dp'), may hold values from -6 to 6
- coarse_gain: float32 [8, 128], replicated, may hold values from 0.5 to 1
Outputs:
- section_starts: float32 [8, 64, 32, 32, 128], P('layer', 'dp')
- weight_grad: float32 [24, 1152, 128], P('layer', 'dp')
- bias_grad: float32 [24, 128], P('layer', 'dp')
The draws below stay inside these ranges and needn't reach their ends.
All inputs are finite; a program needn't handle non-finite values.
Results may differ from the reference program's by a relative error of at most 0.007.
Values sent between devices are 32-bit elements; how exact they have to be, the bound alone decides.
No kernel may reach another device: no remote copies, remote signals or barrier semaphores. Data moves between devices by JAX's collectives and lax.ppermute only.
A program may use at most 64 MiB of HBM per device.

```python
import math
import jax
import jax.numpy as jnp
from jax import lax

CH = 128
HGT = 32
WID = 32
L_SEC = 3
SECTIONS = 8
LAYERS = 24
IMAGES = 64


def raised(array, key, source, target, blocks, factor):
    def block_of(dim):
        return (jnp.arange(array.shape[dim]) // (array.shape[dim] // blocks)).reshape((-1,) + (1,) * (array.ndim - 1 - dim))

    one_side = jax.random.permutation(key, blocks)[block_of(target)]
    second = (block_of(target) + blocks // 2) % blocks
    return jnp.where((block_of(source) == one_side) | (block_of(source) == second), factor * array, array)


def shard_levels(rng, dims, shards, low, top_value):
    def one(axis_at, parts):
        steps = jax.random.uniform(jax.random.fold_in(jax.random.fold_in(rng, 6), axis_at), (parts,), jnp.float32, low / len(shards), top_value / len(shards))
        return jnp.repeat(jnp.exp(steps), dims[axis_at] // parts).reshape((-1,) + (1,) * (len(dims) - axis_at - 1))

    gain = one(*shards[0])
    for cut in shards[1:]:
        gain = gain * one(*cut)
    return gain


def noise(key, dims, scale, most, pieces=(), kind=jnp.bfloat16):
    loudness = shard_levels(key, dims, pieces, -0.22, 0.18) if pieces else 1.0
    drawn = jax.random.normal(key, dims, jnp.float32) * scale * loudness
    return jnp.minimum(jnp.maximum(drawn, -most), most).astype(kind)


def noise_with(rng, extent, width, bound, shards, heavy, held_as=jnp.bfloat16):
    result = width * jax.random.normal(rng, extent, jnp.float32)
    if shards:
        result = result * shard_levels(rng, extent, shards, -0.22, 0.18)
    return jnp.clip(raised(result, jax.random.fold_in(rng, 3), *heavy), -bound, bound).astype(held_as)


def setup_inputs(seed: int = 0) -> dict:
    splits = jax.random.split(jax.random.key(seed), 6)
    return {
        "states": noise_with(splits[0], (LAYERS, IMAGES, HGT, WID, CH), 1.0, 6.0, ((0, 8), (1, 32)), (1, 4, 32, 2.75)),
        "weights": noise(splits[1], (LAYERS, 9 * CH, CH), (9 * CH) ** -0.5, 0.1875, ((0, 8),)),
        "bias": noise(splits[2], (LAYERS, CH), 0.5, 3.0, ((0, 8),), jnp.float32),
        "guesses": noise(splits[3], (SECTIONS, IMAGES, HGT, WID, CH), 1.0, 6.0, ((0, 8), (1, 32)), jnp.float32),
        "coarse_gain": jnp.clip(jnp.exp(jax.random.uniform(splits[4], (SECTIONS, CH), jnp.float32, math.log(0.5), math.log(1.0))), 0.5, 1.0),
    }


step_size = 0.5
layout_names = ("NHWC", "HWIO", "NHWC")


def as_kernel(matrix):
    channels = matrix.shape[1]
    return matrix.reshape(3, 3, channels, channels)


def convolve(field, kernel):
    return lax.conv_general_dilated(field, kernel, (1, 1), ((1, 1), (1, 1)), dimension_numbers=layout_names, preferred_element_type=jnp.float32)


def transpose_conv(scaled, matrix):
    kernel = jnp.swapaxes(as_kernel(matrix)[::-1, ::-1], 2, 3)
    return convolve(scaled, kernel)


def weight_term(field, scaled):
    height = field.shape[1]
    breadth = field.shape[2]
    padded = jnp.pad(field, ((0, 0), (1, 1), (1, 1), (0, 0)))
    blocks = []
    for row_tap in range(3):
        for col_tap in range(3):
            window = padded[:, row_tap:row_tap + height, col_tap:col_tap + breadth, :]
            blocks.append(lax.dot_general(window, scaled, (((0, 1, 2), (0, 1, 2)), ((), ())), preferred_element_type=jnp.float32))
    return jnp.concatenate(blocks, axis=0)


def slopes(field, matrix, offset):
    value = jnp.tanh(convolve(field, as_kernel(matrix)) + offset)
    return 1.0 - value * value


def reference(states, weights, bias, guesses, coarse_gain):
    scale = step_size / IMAGES
    derivs = [slopes(states[layer], weights[layer], bias[layer]) for layer in range(LAYERS)]
    firsts = []
    for section in range(SECTIONS):
        adjoint = guesses[section]
        for position in reversed(range(L_SEC)):
            layer = section * L_SEC + position
            scaled = (derivs[layer] * adjoint).astype(jnp.bfloat16)
            adjoint = adjoint + step_size * transpose_conv(scaled, weights[layer])
        firsts.append(adjoint)
    carried = jnp.zeros_like(guesses[0])
    corrections = [carried] * SECTIONS
    for section in range(SECTIONS - 2, -1, -1):
        carried = (firsts[section + 1] - guesses[section]) + coarse_gain[section] * carried
        corrections[section] = carried
    starts = []
    weight_rows = [None] * LAYERS
    bias_rows = [None] * LAYERS
    for section in range(SECTIONS):
        adjoint = guesses[section] + corrections[section]
        for position in reversed(range(L_SEC)):
            layer = section * L_SEC + position
            scaled = (derivs[layer] * adjoint).astype(jnp.bfloat16)
            adjoint = adjoint + step_size * transpose_conv(scaled, weights[layer])
            weight_rows[layer] = scale * weight_term(states[layer], scaled)
            bias_rows[layer] = scale * jnp.sum(scaled, axis=(0, 1, 2), dtype=jnp.float32)
        starts.append(adjoint)
    return jnp.stack(starts), jnp.stack(weight_rows), jnp.stack(bias_rows)
```

```python
import functools

import jax
import jax.numpy as jnp
from jax import lax
from jax.experimental import pallas as pl
from jax.experimental.pallas import tpu as pltpu
from jax.sharding import PartitionSpec as P

CH = 128
SIDE = 32
PAIRS = SIDE // 2
DEPTH = 3
TAPS = 9 * CH
TRIPLE = 3 * CH
STEP = 0.5
BLOCK = 8
CHUNKS = PAIRS // BLOCK
ROWS = 36
SLAB = 40
f32 = jnp.float32
bf16 = jnp.bfloat16


def dot(a, b):
    return jnp.dot(a, b, preferred_element_type=f32)


def for_chunks(images, body):
    def one(at, carry):
        body(at // CHUNKS, (at % CHUNKS) * BLOCK)
        return carry

    lax.fori_loop(0, images * CHUNKS, one, 0)


def clear_edges(ref):
    images = ref.shape[0]
    zero = jnp.zeros((images, 1, SIDE, TRIPLE), bf16)
    ref[:, 0:1, :, 0:TRIPLE] = zero
    ref[:, PAIRS : PAIRS + 1, :, TRIPLE:] = zero


def spread(ref, image, pair, half, value):
    rows = value.shape[0]
    column = lax.broadcasted_iota(jnp.int32, value.shape, 0) & (SIDE - 1)
    left = jnp.where(column == 0, 0.0, pltpu.roll(value, 1, 0))
    right = jnp.where(column == SIDE - 1, 0.0, pltpu.roll(value, rows - 1, 0))
    base = (1 - half) * TRIPLE
    for at, part in enumerate((left, value, right)):
        lanes = slice(base + at * CH, base + (at + 1) * CH)
        ref[image, pl.ds(pair + half, rows // SIDE), :, lanes] = part.astype(bf16).reshape(-1, SIDE, CH)


def convolve(ref, image, pair, kernel):
    upper = ref[image, pl.ds(pair, BLOCK)].reshape(BLOCK * SIDE, 2 * TRIPLE)
    lower = ref[image, pl.ds(pair + 1, BLOCK)].reshape(BLOCK * SIDE, 2 * TRIPLE)
    return dot(upper, kernel[0 : 2 * TRIPLE, :]) + dot(lower, kernel[2 * TRIPLE :, :])


def fill_kernels(weights, layer, forward, adjoint):
    zero = jnp.zeros((TRIPLE, CH), bf16)
    for row in range(4):
        for half in range(2):
            lanes = slice(half * CH, (half + 1) * CH)
            tap = row - half
            if not 0 <= tap <= 2:
                if forward is not None:
                    forward[row * TRIPLE : (row + 1) * TRIPLE, lanes] = zero
                adjoint[layer, row * TRIPLE : (row + 1) * TRIPLE, lanes] = zero
            elif forward is not None:
                forward[row * TRIPLE : (row + 1) * TRIPLE, lanes] = weights[
                    layer, tap * TRIPLE : (tap + 1) * TRIPLE, :
                ]
    for tap in range(3):
        for side in range(3):
            source = ((2 - tap) * 3 + 2 - side) * CH
            turned = weights[layer, source : source + CH, :].T
            for half in range(2):
                row = (tap + half) * TRIPLE + side * CH
                adjoint[layer, row : row + CH, half * CH : (half + 1) * CH] = turned


def first_kernel(
    states, weights, bias, guess, gain, sent, slope, adjoint_kernels, field, patches, forward, adjoint
):
    images = guess.shape[0]
    clear_edges(field)
    clear_edges(patches)
    for layer in reversed(range(DEPTH)):
        fill_kernels(weights, layer, forward, adjoint_kernels)
        offset = bias[layer : layer + 1, :]

        def gather(image, pair):
            for half in range(2):
                value = states[layer, image, pl.ds(pair, BLOCK), half].reshape(BLOCK * SIDE, CH)
                spread(field, image, pair, half, value.astype(f32))

        for_chunks(images, gather)

        def derive(image, pair):
            both = convolve(field, image, pair, forward)
            for half in range(2):
                lanes = slice(half * CH, (half + 1) * CH)
                value = jnp.tanh(both[:, lanes] + offset)
                value = 1.0 - value * value
                slope[layer, image, pl.ds(pair, BLOCK), :, lanes] = value.reshape(BLOCK, SIDE, CH)
                if layer == DEPTH - 1:
                    now = guess[image, pl.ds(pair, BLOCK), half]
                else:
                    now = adjoint[image, pl.ds(pair, BLOCK), :, lanes]
                spread(patches, image, pair, half, value * now.reshape(BLOCK * SIDE, CH))

        for_chunks(images, derive)

        def back(image, pair):
            both = convolve(patches, image, pair, adjoint_kernels.at[layer])
            for half in range(2):
                lanes = slice(half * CH, (half + 1) * CH)
                change = STEP * both[:, lanes].reshape(BLOCK, SIDE, CH)
                if layer == DEPTH - 1:
                    now = guess[image, pl.ds(pair, BLOCK), half]
                else:
                    now = adjoint[image, pl.ds(pair, BLOCK), :, lanes]
                if layer:
                    adjoint[image, pl.ds(pair, BLOCK), :, lanes] = now + change
                else:
                    old = guess[image, pl.ds(pair, BLOCK), half]
                    sent[image, pl.ds(pair, BLOCK), half] = now + change - gain[...].reshape(1, 1, CH) * old

        for_chunks(images, back)


def second_kernel(
    flags, states, guess, begun, slope, adjoint_kernels, start, mine, other, patches, adjoint, grads, sums, scale
):
    images = guess.shape[0]
    clear_edges(patches)
    last = flags[0] != 0
    core = flags[1]
    for layer in reversed(range(DEPTH)):
        sums[...] = jnp.zeros_like(sums)

        def derive(image, pair):
            for half in range(2):
                lanes = slice(half * CH, (half + 1) * CH)
                if layer == DEPTH - 1:
                    now = jnp.where(
                        last, guess[image, pl.ds(pair, BLOCK), half], begun[image, pl.ds(pair, BLOCK), half]
                    )
                    adjoint[image, pl.ds(pair, BLOCK), :, lanes] = now
                else:
                    now = adjoint[image, pl.ds(pair, BLOCK), :, lanes]
                value = slope[layer, image, pl.ds(pair, BLOCK), :, lanes] * now
                value = value.reshape(BLOCK * SIDE, CH).astype(bf16).astype(f32)
                sums[...] += value.reshape(-1, 8, CH).sum(axis=0)
                spread(patches, image, pair, half, value)

        for_chunks(images, derive)

        def back(image, pair):
            both = convolve(patches, image, pair, adjoint_kernels.at[layer])
            for half in range(2):
                lanes = slice(half * CH, (half + 1) * CH)
                change = STEP * both[:, lanes].reshape(BLOCK, SIDE, CH)
                now = adjoint[image, pl.ds(pair, BLOCK), :, lanes]
                if layer:
                    adjoint[image, pl.ds(pair, BLOCK), :, lanes] = now + change
                else:
                    start[image, pl.ds(pair, BLOCK), half] = now + change

        for_chunks(images, back)

        points = images * PAIRS * SIDE
        halves = [states[layer, :, :, half].reshape(points, CH) for half in range(2)]
        field = jnp.concatenate(halves, axis=1)
        for group in range(2):
            for third in range(3):
                lanes = slice(third * 2 * CH, (third + 1) * 2 * CH)
                part = patches[:, group : group + PAIRS, :, lanes].reshape(points, 2 * CH)
                result = lax.dot_general(field, part, (((0,), (0,)), ((), ())), preferred_element_type=f32)
                for piece in range(2):
                    at = third * 2 + piece
                    row, side = divmod(at, 3)
                    for half in range(2):
                        tap = row + 2 * group - half
                        if not 0 <= tap <= 2:
                            continue
                        block = ((2 - tap) * 3 + 2 - side) * CH
                        value = result[half * CH : (half + 1) * CH, piece * CH : (piece + 1) * CH] * scale
                        fresh = (group, row, half) in ((0, 0, 0), (0, 1, 0), (1, 0, 0))
                        if fresh:
                            grads[block : block + CH, :] = value
                        else:
                            grads[block : block + CH, :] += value
        total = scale * jnp.sum(sums[...], axis=0, keepdims=True)
        tail = jnp.broadcast_to(total, (SLAB - ROWS, CH))
        for chip in range(16):
            even = jnp.concatenate([grads[chip * 72 : chip * 72 + 36, :], tail], axis=0)
            odd = jnp.concatenate([grads[chip * 72 + 36 : chip * 72 + 72, :], tail], axis=0)
            mine[chip, layer] = jnp.where(core == 0, even, odd)
            other[chip, layer] = jnp.where(core == 0, odd, even)


def limits():
    return pltpu.CompilerParams(vmem_limit_bytes=56 * 1024 * 1024)


def run_first(states, weights, bias, guess, gain):
    images = guess.shape[0]
    pair_shape = (images, PAIRS, SIDE, 2 * CH)
    patch_shape = (images, PAIRS + 1, SIDE, 2 * TRIPLE)
    return pl.pallas_call(
        first_kernel,
        out_shape=(
            jax.ShapeDtypeStruct(guess.shape, f32),
            jax.ShapeDtypeStruct((DEPTH, *pair_shape), f32),
            jax.ShapeDtypeStruct((DEPTH, 4 * TRIPLE, 2 * CH), bf16),
        ),
        scratch_shapes=[
            pltpu.VMEM(patch_shape, bf16),
            pltpu.VMEM(patch_shape, bf16),
            pltpu.VMEM((4 * TRIPLE, 2 * CH), bf16),
            pltpu.VMEM(pair_shape, f32),
        ],
        compiler_params=limits(),
        name="first_relaxation",
    )(states, weights, bias, guess, gain)


def run_second(flags, states, guess, begun, slope, adjoint_kernels, scale):
    images = guess.shape[0]
    pair_shape = (images, PAIRS, SIDE, 2 * CH)
    patch_shape = (images, PAIRS + 1, SIDE, 2 * TRIPLE)
    vmem = pl.BlockSpec(memory_space=pltpu.VMEM)
    return pl.pallas_call(
        functools.partial(second_kernel, scale=scale),
        out_shape=(
            jax.ShapeDtypeStruct(guess.shape, f32),
            jax.ShapeDtypeStruct((16, DEPTH, SLAB, CH), f32),
            jax.ShapeDtypeStruct((16, DEPTH, SLAB, CH), f32),
        ),
        in_specs=[pl.BlockSpec(memory_space=pltpu.SMEM)] + [vmem] * 5,
        scratch_shapes=[
            pltpu.VMEM(patch_shape, bf16),
            pltpu.VMEM(pair_shape, f32),
            pltpu.VMEM((TAPS, CH), f32),
            pltpu.VMEM((8, CH), f32),
        ],
        compiler_params=limits(),
        name="second_relaxation",
    )(flags, states, guess, begun, slope, adjoint_kernels)


def scatter_sum(mine, other):
    index = lax.axis_index("dp")
    along_x, along_z = index // 8, (index // 2) % 4
    total = mine + lax.ppermute(other, "dp", [(at, at ^ 1) for at in range(32)])

    def stage(parts, place, shift):
        received = []
        for hop in range(1, 4):
            pairs = [(at, shift(at, hop)) for at in range(32)]
            part = lax.dynamic_index_in_dim(parts, (place + hop) % 4, 0, False)
            received.append(lax.ppermute(part, "dp", pairs))
        return lax.dynamic_index_in_dim(parts, place, 0, False) + received[0] + received[1] + received[2]

    total = total.reshape(4, 4, DEPTH, SLAB, CH)
    total = stage(total, along_x, lambda at, hop: (at // 8 + hop) % 4 * 8 + at % 8)
    return stage(total, along_z, lambda at, hop: at // 8 * 8 + (at // 2 + hop) % 4 * 2 + at % 2)


def per_device(states, weights, bias, guesses, coarse_gain):
    section = lax.axis_index("layer")
    sections = lax.axis_size("layer")
    images = states.shape[1]
    scale = STEP / (images * lax.axis_size("dp"))
    paired = (images, PAIRS, 2, SIDE, CH)
    states = states.reshape(DEPTH, *paired)
    guess = guesses.reshape(paired)
    before = lax.dynamic_slice_in_dim(coarse_gain, jnp.maximum(section - 1, 0), 1, 0)
    inside = (section > 0) & (section < sections - 1)
    before = jnp.where(inside, before, 0.0)
    sent, slope, adjoint_kernels = run_first(states, weights, bias, guess, before)

    parts = lax.all_to_all(sent.reshape(sections, -1, CH), "layer", 0, 0)
    carried = parts[sections - 1]
    begun = [carried, carried]
    for at in range(sections - 2, 0, -1):
        carried = parts[at] + coarse_gain[at - 1] * carried
        begun.append(carried)
    begun = jnp.stack(begun[::-1])
    begun = lax.all_to_all(begun, "layer", 0, 0).reshape(paired)

    flags = jnp.stack([(section == sections - 1).astype(jnp.int32), (lax.axis_index("dp") % 2).astype(jnp.int32)])
    start, mine, other = run_second(flags, states, guess, begun, slope, adjoint_kernels, scale)
    total = scatter_sum(mine, other)
    bias_grad = lax.dynamic_slice_in_dim(total[:, ROWS, :], lax.axis_index("dp") * 4, 4, 1)
    return start.reshape(guesses.shape), total[:, :ROWS, :], bias_grad


def solution(mesh):
    return jax.shard_map(
        per_device,
        mesh=mesh,
        in_specs=(
            P("layer", "dp", None, None, None),
            P("layer", None, None),
            P("layer", None),
            P("layer", "dp", None, None, None),
            P(),
        ),
        out_specs=(P("layer", "dp", None, None, None), P("layer", "dp", None), P("layer", "dp")),
        check_vma=False,
    )
```

```python
import functools

import jax
import jax.numpy as jnp
from jax import lax
from jax.experimental import pallas as pl
from jax.experimental.pallas import tpu as pltpu
from jax.sharding import PartitionSpec as P

CH = 128
SIDE = 32
PAIRS = SIDE // 2
DEPTH = 3
TAPS = 9 * CH
TRIPLE = 3 * CH
STEP = 0.5
BLOCK = PAIRS
FINE = 4
ROWS = 36
SLAB = 40
f32 = jnp.float32
bf16 = jnp.bfloat16


def dot(a, b):
    return jnp.dot(a, b, preferred_element_type=f32)


def for_steps(images, body):
    steps = PAIRS // FINE

    def one(at, carry):
        body(at // steps, (at % steps) * FINE)
        return carry

    lax.fori_loop(0, images * steps, one, 0)


def clear_edges(ref):
    images = ref.shape[0]
    zero = jnp.zeros((images, 1, SIDE, TRIPLE), bf16)
    ref[:, 0:1, :, 0:TRIPLE] = zero
    ref[:, PAIRS : PAIRS + 1, :, TRIPLE:] = zero


def spread(ref, image, pair, half, value):
    rows = value.shape[0]
    column = lax.broadcasted_iota(jnp.int32, value.shape, 0) & (SIDE - 1)
    left = jnp.where(column == 0, 0.0, pltpu.roll(value, 1, 0))
    right = jnp.where(column == SIDE - 1, 0.0, pltpu.roll(value, rows - 1, 0))
    base = (1 - half) * TRIPLE
    for at, part in enumerate((left, value, right)):
        lanes = slice(base + at * CH, base + (at + 1) * CH)
        ref[image, pl.ds(pair + half, rows // SIDE), :, lanes] = part.astype(bf16).reshape(-1, SIDE, CH)


def convolve(ref, image, pair, kernel):
    upper = ref[image, pl.ds(pair, BLOCK)].reshape(BLOCK * SIDE, 2 * TRIPLE)
    lower = ref[image, pl.ds(pair + 1, BLOCK)].reshape(BLOCK * SIDE, 2 * TRIPLE)
    top, middle, bottom = (kernel[at * TRIPLE : (at + 1) * TRIPLE, :] for at in range(3))
    zero = jnp.zeros((TRIPLE, CH), bf16)

    def beside(left, right):
        return jnp.concatenate([jnp.concatenate(left, axis=0), jnp.concatenate(right, axis=0)], axis=1)

    return dot(upper, beside((top, middle), (zero, top))) + dot(lower, beside((bottom, zero), (middle, bottom)))


def gather(states, field, layer, image, pair, count):
    for half in range(2):
        value = states[layer, image, pl.ds(pair, count), half].reshape(count * SIDE, CH)
        spread(field, image, pair, half, value.astype(f32))


def first_kernel(
    states_from, weights_from, bias, guess_from, gain, flags,
    sent, slope_to, turned_to,
    states, weights, guess, slope, turned, field, patches, adjoint, came, left,
):
    images = guess.shape[0]
    arrivals = {}
    for layer in reversed(range(DEPTH)):
        arrivals[layer] = [
            pltpu.make_async_copy(states_from.at[layer], states.at[layer], came.at[layer]),
            pltpu.make_async_copy(weights_from.at[layer], weights.at[layer], came.at[DEPTH + layer]),
        ]
        for copy in arrivals[layer]:
            copy.start()
        if layer == DEPTH - 1:
            guess_copy = pltpu.make_async_copy(guess_from, guess, came.at[2 * DEPTH])
            guess_copy.start()
    departures = []
    clear_edges(field)
    clear_edges(patches)
    section, sections = flags[0], flags[1]
    inside = (section > 0) & (section < sections - 1)
    before = jnp.where(inside, gain[pl.ds(jnp.maximum(section - 1, 0), 1), :], 0.0).reshape(1, 1, CH)
    for layer in reversed(range(DEPTH)):
        last = layer == DEPTH - 1
        if last:
            for copy in arrivals[layer]:
                copy.wait()
            for_steps(images, lambda image, pair: gather(states, field, layer, image, pair, FINE))
        for tap in range(9):
            source = (8 - tap) * CH
            turned[layer, tap * CH : (tap + 1) * CH, :] = weights[layer, source : source + CH, :].T
        copy = pltpu.make_async_copy(turned.at[layer], turned_to.at[layer], left.at[DEPTH + layer])
        copy.start()
        departures.append(copy)
        if last:
            guess_copy.wait()
        offset = bias[layer : layer + 1, :]
        for image in range(images):
            both = convolve(field, image, 0, weights.at[layer])
            for half in range(2):
                lanes = slice(half * CH, (half + 1) * CH)
                value = jnp.tanh(both[:, lanes] + offset)
                value = 1.0 - value * value
                slope[layer, image, :, :, lanes] = value.reshape(PAIRS, SIDE, CH)
                now = guess[image, :, half] if last else adjoint[image, :, :, lanes]
                spread(patches, image, 0, half, value * now.reshape(PAIRS * SIDE, CH))
        copy = pltpu.make_async_copy(slope.at[layer], slope_to.at[layer], left.at[layer])
        copy.start()
        departures.append(copy)
        if layer:
            for copy in arrivals[layer - 1]:
                copy.wait()
        for image in range(images):
            both = convolve(patches, image, 0, turned.at[layer])
            for half in range(2):
                lanes = slice(half * CH, (half + 1) * CH)
                change = STEP * both[:, lanes].reshape(PAIRS, SIDE, CH)
                now = guess[image, :, half] if last else adjoint[image, :, :, lanes]
                if layer:
                    adjoint[image, :, :, lanes] = now + change
                else:
                    sent[image, :, half] = now + change - before * guess[image, :, half]
            if layer:
                gather(states, field, layer - 1, image, 0, PAIRS)
    for copy in departures:
        copy.wait()


def second_kernel(
    states_from, guess_from, begun, slope_from, turned_from, flags,
    start, mine, other,
    states, guess, slope, turned, patches, adjoint, grads, sums, came, scale,
):
    images = guess.shape[0]
    arrivals = {}
    for layer in reversed(range(DEPTH)):
        arrivals[layer] = [
            pltpu.make_async_copy(source.at[layer], to.at[layer], came.at[at * DEPTH + layer])
            for at, (source, to) in enumerate(((slope_from, slope), (turned_from, turned), (states_from, states)))
        ]
    guess_copy = pltpu.make_async_copy(guess_from, guess, came.at[3 * DEPTH])
    guess_copy.start()
    for layer in reversed(range(DEPTH)):
        for copy in arrivals[layer]:
            copy.start()
    clear_edges(patches)
    last = flags[0] == flags[1] - 1
    core = flags[2]
    guess_copy.wait()
    for layer in reversed(range(DEPTH)):
        sums[...] = jnp.zeros_like(sums)
        arrivals[layer][0].wait()

        def derive(image, pair):
            for half in range(2):
                lanes = slice(half * CH, (half + 1) * CH)
                if layer == DEPTH - 1:
                    now = jnp.where(
                        last, guess[image, pl.ds(pair, FINE), half], begun[image, pl.ds(pair, FINE), half]
                    )
                    adjoint[image, pl.ds(pair, FINE), :, lanes] = now
                else:
                    now = adjoint[image, pl.ds(pair, FINE), :, lanes]
                value = slope[layer, image, pl.ds(pair, FINE), :, lanes] * now
                value = value.reshape(FINE * SIDE, CH).astype(bf16).astype(f32)
                sums[...] += value.reshape(-1, 8, CH).sum(axis=0)
                spread(patches, image, pair, half, value)

        for_steps(images, derive)
        arrivals[layer][1].wait()
        for image in range(images):
            both = convolve(patches, image, 0, turned.at[layer])
            for half in range(2):
                lanes = slice(half * CH, (half + 1) * CH)
                change = STEP * both[:, lanes].reshape(PAIRS, SIDE, CH)
                now = adjoint[image, :, :, lanes]
                if layer:
                    adjoint[image, :, :, lanes] = now + change
                else:
                    start[image, :, half] = now + change
        arrivals[layer][2].wait()

        points = images * PAIRS * SIDE
        halves = [states[layer, :, :, half].reshape(points, CH) for half in range(2)]
        field = jnp.concatenate(halves, axis=1)
        for group in range(2):
            for third in range(3):
                lanes = slice(third * 2 * CH, (third + 1) * 2 * CH)
                part = patches[:, group : group + PAIRS, :, lanes].reshape(points, 2 * CH)
                result = lax.dot_general(field, part, (((0,), (0,)), ((), ())), preferred_element_type=f32)
                for piece in range(2):
                    row, side = divmod(third * 2 + piece, 3)
                    for half in range(2):
                        tap = row + 2 * group - half
                        if not 0 <= tap <= 2:
                            continue
                        block = ((2 - tap) * 3 + 2 - side) * CH
                        value = result[half * CH : (half + 1) * CH, piece * CH : (piece + 1) * CH] * scale
                        if (group, row, half) in ((0, 0, 0), (0, 1, 0), (1, 0, 0)):
                            grads[block : block + CH, :] = value
                        else:
                            grads[block : block + CH, :] += value
        total = scale * jnp.sum(sums[...], axis=0, keepdims=True)
        tail = jnp.broadcast_to(total, (SLAB - ROWS, CH))
        for chip in range(16):
            even = jnp.concatenate([grads[chip * 72 : chip * 72 + 36, :], tail], axis=0)
            odd = jnp.concatenate([grads[chip * 72 + 36 : chip * 72 + 72, :], tail], axis=0)
            mine[chip, layer] = jnp.where(core == 0, even, odd)
            other[chip, layer] = jnp.where(core == 0, odd, even)


def middle_kernel(parts, gain, begun):
    count = parts.shape[0]
    carried = parts[count - 1]
    begun[count - 1] = carried
    begun[count - 2] = carried
    for at in range(count - 2, 0, -1):
        carried = parts[at] + gain[at - 1 : at, :] * carried
        begun[at - 1] = carried


ANY = pl.BlockSpec(memory_space=pltpu.HBM)
VMEM = pl.BlockSpec(memory_space=pltpu.VMEM)
SMEM = pl.BlockSpec(memory_space=pltpu.SMEM)


def limits(mib):
    return pltpu.CompilerParams(vmem_limit_bytes=mib * 1024 * 1024)


def run_first(states, weights, bias, guess, gain, flags):
    images = guess.shape[0]
    pair_shape = (images, PAIRS, SIDE, 2 * CH)
    patch_shape = (images, PAIRS + 1, SIDE, 2 * TRIPLE)
    slope = (DEPTH, *pair_shape)
    return pl.pallas_call(
        first_kernel,
        out_shape=(
            jax.ShapeDtypeStruct(guess.shape, f32),
            jax.ShapeDtypeStruct(slope, f32),
            jax.ShapeDtypeStruct(weights.shape, bf16),
        ),
        in_specs=[ANY, ANY, VMEM, ANY, VMEM, SMEM],
        out_specs=(VMEM, ANY, ANY),
        scratch_shapes=[
            pltpu.VMEM(states.shape, bf16),
            pltpu.VMEM(weights.shape, bf16),
            pltpu.VMEM(guess.shape, f32),
            pltpu.VMEM(slope, f32),
            pltpu.VMEM(weights.shape, bf16),
            pltpu.VMEM(patch_shape, bf16),
            pltpu.VMEM(patch_shape, bf16),
            pltpu.VMEM(pair_shape, f32),
            pltpu.SemaphoreType.DMA((2 * DEPTH + 1,)),
            pltpu.SemaphoreType.DMA((2 * DEPTH,)),
        ],
        compiler_params=limits(60),
        name="first_relaxation",
    )(states, weights, bias, guess, gain, flags)


def run_middle(parts, gain):
    return pl.pallas_call(
        middle_kernel,
        out_shape=jax.ShapeDtypeStruct(parts.shape, f32),
        in_specs=[VMEM, VMEM],
        out_specs=VMEM,
        name="recurrence",
    )(parts, gain)


def run_second(states, guess, begun, slope, turned, flags, scale):
    images = guess.shape[0]
    pair_shape = (images, PAIRS, SIDE, 2 * CH)
    patch_shape = (images, PAIRS + 1, SIDE, 2 * TRIPLE)
    slabs = jax.ShapeDtypeStruct((16, DEPTH, SLAB, CH), f32)
    return pl.pallas_call(
        functools.partial(second_kernel, scale=scale),
        out_shape=(jax.ShapeDtypeStruct(guess.shape, f32), slabs, slabs),
        in_specs=[ANY, ANY, VMEM, ANY, ANY, SMEM],
        out_specs=(VMEM, VMEM, VMEM),
        scratch_shapes=[
            pltpu.VMEM(states.shape, bf16),
            pltpu.VMEM(guess.shape, f32),
            pltpu.VMEM(slope.shape, f32),
            pltpu.VMEM(turned.shape, bf16),
            pltpu.VMEM(patch_shape, bf16),
            pltpu.VMEM(pair_shape, f32),
            pltpu.VMEM((TAPS, CH), f32),
            pltpu.VMEM((8, CH), f32),
            pltpu.SemaphoreType.DMA((3 * DEPTH + 1,)),
        ],
        compiler_params=limits(60),
        name="second_relaxation",
    )(states, guess, begun, slope, turned, flags)


def scatter_sum(mine, other):
    index = lax.axis_index("dp")
    along_x, along_z = index // 8, (index // 2) % 4
    total = mine + lax.ppermute(other, "dp", [(at, at ^ 1) for at in range(32)])

    def stage(parts, place, shift):
        received = []
        for hop in range(1, 4):
            pairs = [(at, shift(at, hop)) for at in range(32)]
            part = lax.dynamic_index_in_dim(parts, (place + hop) % 4, 0, False)
            received.append(lax.ppermute(part, "dp", pairs))
        return lax.dynamic_index_in_dim(parts, place, 0, False) + received[0] + received[1] + received[2]

    total = total.reshape(4, 4, DEPTH, SLAB, CH)
    total = stage(total, along_x, lambda at, hop: (at // 8 + hop) % 4 * 8 + at % 8)
    return stage(total, along_z, lambda at, hop: at // 8 * 8 + (at // 2 + hop) % 4 * 2 + at % 2)


def per_device(states, weights, bias, guesses, coarse_gain):
    section = lax.axis_index("layer")
    sections = lax.axis_size("layer")
    images = states.shape[1]
    scale = STEP / (images * lax.axis_size("dp"))
    paired = (images, PAIRS, 2, SIDE, CH)
    states = states.reshape(DEPTH, *paired)
    guess = guesses.reshape(paired)
    flags = jnp.stack([section, jnp.int32(sections), lax.axis_index("dp") % 2]).astype(jnp.int32)
    sent, slope, turned = run_first(states, weights, bias, guess, coarse_gain, flags)

    parts = lax.all_to_all(sent.reshape(sections, -1, CH), "layer", 0, 0)
    begun = run_middle(parts, coarse_gain)
    begun = lax.all_to_all(begun, "layer", 0, 0).reshape(paired)

    start, mine, other = run_second(states, guess, begun, slope, turned, flags, scale)
    total = scatter_sum(mine, other)
    bias_grad = lax.dynamic_slice_in_dim(total[:, ROWS, :], lax.axis_index("dp") * 4, 4, 1)
    return start.reshape(guesses.shape), total[:, :ROWS, :], bias_grad


def solution(mesh):
    return jax.shard_map(
        per_device,
        mesh=mesh,
        in_specs=(
            P("layer", "dp", None, None, None),
            P("layer", None, None),
            P("layer", None),
            P("layer", "dp", None, None, None),
            P(),
        ),
        out_specs=(P("layer", "dp", None, None, None), P("layer", "dp", None), P("layer", "dp")),
        check_vma=False,
    )
```

```python
import functools

import jax
import jax.numpy as jnp
from jax import lax
from jax.experimental import pallas as pl
from jax.experimental.pallas import tpu as pltpu
from jax.sharding import PartitionSpec as P

CH = 128
SIDE = 32
PAIRS = SIDE // 2
DEPTH = 3
TAPS = 9 * CH
TRIPLE = 3 * CH
STEP = 0.5
BLOCK = PAIRS
FINE = 4
ROWS = 36
SLAB = 40
f32 = jnp.float32
bf16 = jnp.bfloat16


def dot(a, b):
    return jnp.dot(a, b, preferred_element_type=f32)


def for_steps(images, body):
    steps = PAIRS // FINE

    def one(at, carry):
        body(at // steps, (at % steps) * FINE)
        return carry

    lax.fori_loop(0, images * steps, one, 0)


def clear_edges(ref):
    images = ref.shape[0]
    zero = jnp.zeros((images, 1, SIDE, TRIPLE), bf16)
    ref[:, 0:1, :, 0:TRIPLE] = zero
    ref[:, PAIRS : PAIRS + 1, :, TRIPLE:] = zero


def spread(ref, image, pair, half, value):
    rows = value.shape[0]
    column = lax.broadcasted_iota(jnp.int32, value.shape, 0) & (SIDE - 1)
    left = jnp.where(column == 0, 0.0, pltpu.roll(value, 1, 0))
    right = jnp.where(column == SIDE - 1, 0.0, pltpu.roll(value, rows - 1, 0))
    base = (1 - half) * TRIPLE
    for at, part in enumerate((left, value, right)):
        lanes = slice(base + at * CH, base + (at + 1) * CH)
        ref[image, pl.ds(pair + half, rows // SIDE), :, lanes] = part.astype(bf16).reshape(-1, SIDE, CH)


def convolve(ref, image, pair, kernel):
    upper = ref[image, pl.ds(pair, BLOCK)].reshape(BLOCK * SIDE, 2 * TRIPLE)
    lower = ref[image, pl.ds(pair + 1, BLOCK)].reshape(BLOCK * SIDE, 2 * TRIPLE)
    top, middle, bottom = (kernel[at * TRIPLE : (at + 1) * TRIPLE, :] for at in range(3))
    zero = jnp.zeros((TRIPLE, CH), bf16)

    def beside(left, right):
        return jnp.concatenate([jnp.concatenate(left, axis=0), jnp.concatenate(right, axis=0)], axis=1)

    return dot(upper, beside((top, middle), (zero, top))) + dot(lower, beside((bottom, zero), (middle, bottom)))


def gather(states, field, layer, image, pair, count):
    for half in range(2):
        value = states[layer, image, pl.ds(pair, count), half].reshape(count * SIDE, CH)
        spread(field, image, pair, half, value.astype(f32))


def first_kernel(
    states_from, weights_from, bias, guess_from, gain,
    sent, slope_to, turned_to,
    states, weights, guess, slope, turned, field, patches, adjoint, came, left,
):
    images = guess.shape[0]
    arrivals = {}
    for layer in reversed(range(DEPTH)):
        arrivals[layer] = [
            pltpu.make_async_copy(states_from.at[layer], states.at[layer], came.at[layer]),
            pltpu.make_async_copy(weights_from.at[layer], weights.at[layer], came.at[DEPTH + layer]),
        ]
        for copy in arrivals[layer]:
            copy.start()
        if layer == DEPTH - 1:
            guess_copy = pltpu.make_async_copy(guess_from, guess, came.at[2 * DEPTH])
            guess_copy.start()
    departures = []
    clear_edges(field)
    clear_edges(patches)
    section, sections = lax.axis_index("layer"), lax.axis_size("layer")
    inside = (section > 0) & (section < sections - 1)
    before = jnp.where(inside, gain[pl.ds(jnp.maximum(section - 1, 0), 1), :], 0.0).reshape(1, 1, CH)
    for layer in reversed(range(DEPTH)):
        last = layer == DEPTH - 1
        if last:
            for copy in arrivals[layer]:
                copy.wait()
            for_steps(images, lambda image, pair: gather(states, field, layer, image, pair, FINE))
        for tap in range(9):
            source = (8 - tap) * CH
            turned[layer, tap * CH : (tap + 1) * CH, :] = weights[layer, source : source + CH, :].T
        copy = pltpu.make_async_copy(turned.at[layer], turned_to.at[layer], left.at[DEPTH + layer])
        copy.start()
        departures.append(copy)
        if last:
            guess_copy.wait()
        offset = bias[layer : layer + 1, :]
        for image in range(images):
            both = convolve(field, image, 0, weights.at[layer])
            for half in range(2):
                lanes = slice(half * CH, (half + 1) * CH)
                value = jnp.tanh(both[:, lanes] + offset)
                value = 1.0 - value * value
                slope[layer, image, :, :, lanes] = value.reshape(PAIRS, SIDE, CH)
                now = guess[image, :, half] if last else adjoint[image, :, :, lanes]
                spread(patches, image, 0, half, value * now.reshape(PAIRS * SIDE, CH))
        copy = pltpu.make_async_copy(slope.at[layer], slope_to.at[layer], left.at[layer])
        copy.start()
        departures.append(copy)
        if layer:
            for copy in arrivals[layer - 1]:
                copy.wait()
        for image in range(images):
            both = convolve(patches, image, 0, turned.at[layer])
            for half in range(2):
                lanes = slice(half * CH, (half + 1) * CH)
                change = STEP * both[:, lanes].reshape(PAIRS, SIDE, CH)
                now = guess[image, :, half] if last else adjoint[image, :, :, lanes]
                if layer:
                    adjoint[image, :, :, lanes] = now + change
                else:
                    sent[image, :, half] = now + change - before * guess[image, :, half]
            if layer:
                gather(states, field, layer - 1, image, 0, PAIRS)
    for copy in departures:
        copy.wait()


def start_copies(pairs, semaphores):
    copies = [pltpu.make_async_copy(source, to, semaphores.at[at]) for at, (source, to) in enumerate(pairs)]
    for copy in copies:
        copy.start()
    return copies


def scaled_rows(slope, now, patches, sums, image, pair):
    for half in range(2):
        lanes = slice(half * CH, (half + 1) * CH)
        value = slope[image, pl.ds(pair, FINE), :, lanes] * now(image, pair, half)
        value = value.reshape(FINE * SIDE, CH).astype(bf16).astype(f32)
        if sums is not None:
            sums[...] += value.reshape(-1, 8, CH).sum(axis=0)
        spread(patches, image, pair, half, value)


def weight_products(states, patches, grads, scale, beside=()):
    images = states.shape[0]
    points = images * PAIRS * SIDE
    halves = [states[:, :, half].reshape(points, CH) for half in range(2)]
    field = jnp.concatenate(halves, axis=1)
    beside = list(beside)
    share = -(-len(beside) // 6)
    for group in range(2):
        for third in range(3):
            lanes = slice(third * 2 * CH, (third + 1) * 2 * CH)
            part = patches[:, group : group + PAIRS, :, lanes].reshape(points, 2 * CH)
            only = {(0, 0): 0, (1, 2): 1}.get((group, third))
            left = field if only is None else halves[only]
            result = lax.dot_general(left, part, (((0,), (0,)), ((), ())), preferred_element_type=f32)
            for piece in range(2):
                row, side = divmod(third * 2 + piece, 3)
                for half in range(2) if only is None else (only,):
                    tap = row + 2 * group - half
                    if not 0 <= tap <= 2:
                        continue
                    block = ((2 - tap) * 3 + 2 - side) * CH
                    top = half * CH if only is None else 0
                    value = result[top : top + CH, piece * CH : (piece + 1) * CH] * scale
                    if (group, row, half) in ((0, 0, 0), (0, 1, 0), (1, 0, 0)):
                        grads[block : block + CH, :] = value
                    else:
                        grads[block : block + CH, :] += value
            for step in beside[:share]:
                step()
            beside = beside[share:]


def fill_slabs(grads, sums, scale, at, mine, other):
    core = lax.axis_index("dp") % 2
    total = scale * jnp.sum(sums[...], axis=0, keepdims=True)
    tail = jnp.broadcast_to(total, (SLAB - ROWS, CH))
    for chip in range(16):
        even = jnp.concatenate([grads[chip * 72 : chip * 72 + 36, :], tail], axis=0)
        odd = jnp.concatenate([grads[chip * 72 + 36 : chip * 72 + 72, :], tail], axis=0)
        mine[chip, at] = jnp.where(core == 0, even, odd)
        other[chip, at] = jnp.where(core == 0, odd, even)


def upper_kernel(
    states_from, guess_from, begun, slope_from, turned_from,
    adjoint_to, mine, other,
    states, guess, slope, turned, patches, adjoint, grads, sums, came, left, scale,
):
    images = guess.shape[0]
    (guess_copy,) = start_copies([(guess_from, guess)], came.at[0])
    arrivals = {
        layer: start_copies(
            [
                (slope_from.at[layer], slope.at[layer - 1]),
                (turned_from.at[layer], turned.at[layer - 1]),
                (states_from.at[layer], states.at[layer - 1]),
            ],
            came.at[layer],
        )
        for layer in (2, 1)
    }
    for at in range(2):
        clear_edges(patches.at[at])
    last = lax.axis_index("layer") == lax.axis_size("layer") - 1
    sums[...] = jnp.zeros_like(sums)

    def chosen(image, pair, half):
        now = jnp.where(last, guess[image, pl.ds(pair, FINE), half], begun[image, pl.ds(pair, FINE), half])
        adjoint[image, pl.ds(pair, FINE), :, half * CH : (half + 1) * CH] = now
        return now

    def held(image, pair, half):
        return adjoint[image, pl.ds(pair, FINE), :, half * CH : (half + 1) * CH]

    def back(at):
        for image in range(images):
            both = convolve(patches.at[at], image, 0, turned.at[at])
            for half in range(2):
                lanes = slice(half * CH, (half + 1) * CH)
                change = STEP * both[:, lanes].reshape(PAIRS, SIDE, CH)
                adjoint[image, :, :, lanes] = adjoint[image, :, :, lanes] + change

    guess_copy.wait()
    arrivals[2][0].wait()
    for_steps(images, lambda image, pair: scaled_rows(slope.at[1], chosen, patches.at[1], sums.at[1], image, pair))
    for copy in arrivals[2][1:] + arrivals[1]:
        copy.wait()
    back(1)
    steps = [
        functools.partial(scaled_rows, slope.at[0], held, patches.at[0], sums.at[0], image, pair)
        for image in range(images)
        for pair in range(0, PAIRS, FINE)
    ]
    weight_products(states.at[1], patches.at[1], grads.at[1], scale, steps)
    back(0)
    (away,) = start_copies([(adjoint, adjoint_to)], left)
    weight_products(states.at[0], patches.at[0], grads.at[0], scale)
    for at in range(2):
        fill_slabs(grads.at[at], sums.at[at], scale, at, mine, other)
    away.wait()


def lower_kernel(states_from, adjoint_from, slope_from, mine, other, states, adjoint, slope, patches, grads, sums, came, scale):
    images = adjoint.shape[0]
    copies = start_copies(
        [(slope_from.at[0], slope), (adjoint_from, adjoint), (states_from.at[0], states)], came
    )
    clear_edges(patches)
    sums[...] = jnp.zeros_like(sums)
    for copy in copies:
        copy.wait()

    def held(image, pair, half):
        return adjoint[image, pl.ds(pair, FINE), :, half * CH : (half + 1) * CH]

    for_steps(images, lambda image, pair: scaled_rows(slope, held, patches, sums, image, pair))
    weight_products(states, patches, grads, scale)
    fill_slabs(grads, sums, scale, 0, mine, other)


def start_kernel(adjoint_from, slope_from, turned_from, start, adjoint, slope, turned, patches, came):
    images = adjoint.shape[0]
    copies = start_copies(
        [(slope_from.at[0], slope), (adjoint_from, adjoint), (turned_from.at[0], turned)], came
    )
    clear_edges(patches)
    for copy in copies:
        copy.wait()

    def held(image, pair, half):
        return adjoint[image, pl.ds(pair, FINE), :, half * CH : (half + 1) * CH]

    for_steps(images, lambda image, pair: scaled_rows(slope, held, patches, None, image, pair))
    for image in range(images):
        both = convolve(patches, image, 0, turned)
        for half in range(2):
            lanes = slice(half * CH, (half + 1) * CH)
            change = STEP * both[:, lanes].reshape(PAIRS, SIDE, CH)
            start[image, :, half] = adjoint[image, :, :, lanes] + change


def middle_kernel(parts, gain, begun):
    count = parts.shape[0]
    carried = parts[count - 1]
    begun[count - 1] = carried
    begun[count - 2] = carried
    for at in range(count - 2, 0, -1):
        carried = parts[at] + gain[at - 1 : at, :] * carried
        begun[at - 1] = carried


ANY = pl.BlockSpec(memory_space=pltpu.HBM)
VMEM = pl.BlockSpec(memory_space=pltpu.VMEM)


def limits(mib):
    return pltpu.CompilerParams(vmem_limit_bytes=mib * 1024 * 1024)


def run_first(states, weights, bias, guess, gain):
    images = guess.shape[0]
    pair_shape = (images, PAIRS, SIDE, 2 * CH)
    patch_shape = (images, PAIRS + 1, SIDE, 2 * TRIPLE)
    slope = (DEPTH, *pair_shape)
    return pl.pallas_call(
        first_kernel,
        out_shape=(
            jax.ShapeDtypeStruct(guess.shape, f32),
            jax.ShapeDtypeStruct(slope, f32),
            jax.ShapeDtypeStruct(weights.shape, bf16),
        ),
        in_specs=[ANY, ANY, VMEM, ANY, VMEM],
        out_specs=(VMEM, ANY, ANY),
        scratch_shapes=[
            pltpu.VMEM(states.shape, bf16),
            pltpu.VMEM(weights.shape, bf16),
            pltpu.VMEM(guess.shape, f32),
            pltpu.VMEM(slope, f32),
            pltpu.VMEM(weights.shape, bf16),
            pltpu.VMEM(patch_shape, bf16),
            pltpu.VMEM(patch_shape, bf16),
            pltpu.VMEM(pair_shape, f32),
            pltpu.SemaphoreType.DMA((2 * DEPTH + 1,)),
            pltpu.SemaphoreType.DMA((2 * DEPTH,)),
        ],
        compiler_params=limits(60),
        name="first_relaxation",
    )(states, weights, bias, guess, gain)


def run_middle(parts, gain):
    return pl.pallas_call(
        middle_kernel,
        out_shape=jax.ShapeDtypeStruct(parts.shape, f32),
        in_specs=[VMEM, VMEM],
        out_specs=VMEM,
        compiler_params=limits(8),
        name="recurrence",
    )(parts, gain)


def cost(products, size):
    return pl.CostEstimate(flops=products * 4 * SIDE * SIDE * TAPS * CH, bytes_accessed=size, transcendentals=0)


def slabs(layers):
    return jax.ShapeDtypeStruct((16, layers, SLAB, CH), f32)


def run_upper(states, guess, begun, slope, turned, scale):
    pair_shape, patch_shape = slope.shape[1:], (slope.shape[1], PAIRS + 1, SIDE, 2 * TRIPLE)
    return pl.pallas_call(
        functools.partial(upper_kernel, scale=scale),
        out_shape=(jax.ShapeDtypeStruct(pair_shape, f32), slabs(2), slabs(2)),
        in_specs=[ANY, ANY, VMEM, ANY, ANY],
        out_specs=(ANY, VMEM, VMEM),
        scratch_shapes=[
            pltpu.VMEM((2, *states.shape[1:]), bf16),
            pltpu.VMEM(guess.shape, f32),
            pltpu.VMEM((2, *pair_shape), f32),
            pltpu.VMEM((2, *turned.shape[1:]), bf16),
            pltpu.VMEM((2, *patch_shape), bf16),
            pltpu.VMEM(pair_shape, f32),
            pltpu.VMEM((2, TAPS, CH), f32),
            pltpu.VMEM((2, 8, CH), f32),
            pltpu.SemaphoreType.DMA((3, 3)),
            pltpu.SemaphoreType.DMA((1,)),
        ],
        compiler_params=limits(60),
        cost_estimate=cost(4, 8 << 20),
        name="upper_layers",
    )(states, guess, begun, slope, turned)


def run_lower(states, adjoint, slope, scale):
    patch_shape = (slope.shape[1], PAIRS + 1, SIDE, 2 * TRIPLE)
    return pl.pallas_call(
        functools.partial(lower_kernel, scale=scale),
        out_shape=(slabs(1), slabs(1)),
        in_specs=[ANY, ANY, ANY],
        out_specs=(VMEM, VMEM),
        scratch_shapes=[
            pltpu.VMEM(states.shape[1:], bf16),
            pltpu.VMEM(adjoint.shape, f32),
            pltpu.VMEM(slope.shape[1:], f32),
            pltpu.VMEM(patch_shape, bf16),
            pltpu.VMEM((TAPS, CH), f32),
            pltpu.VMEM((8, CH), f32),
            pltpu.SemaphoreType.DMA((3,)),
        ],
        compiler_params=limits(60),
        cost_estimate=cost(2, 4 << 20),
        name="lower_gradients",
    )(states, adjoint, slope)


def run_start(adjoint, slope, turned, shape):
    patch_shape = (slope.shape[1], PAIRS + 1, SIDE, 2 * TRIPLE)
    return pl.pallas_call(
        start_kernel,
        out_shape=jax.ShapeDtypeStruct(shape, f32),
        in_specs=[ANY, ANY, ANY],
        out_specs=VMEM,
        scratch_shapes=[
            pltpu.VMEM(adjoint.shape, f32),
            pltpu.VMEM(slope.shape[1:], f32),
            pltpu.VMEM(turned.shape[1:], bf16),
            pltpu.VMEM(patch_shape, bf16),
            pltpu.SemaphoreType.DMA((3,)),
        ],
        compiler_params=limits(60),
        cost_estimate=cost(1, 4 << 20),
        name="section_start",
    )(adjoint, slope, turned)


def add_cores(mine, other):
    return mine + lax.ppermute(other, "dp", [(at, at ^ 1) for at in range(32)])


def add_stage(parts, place, shift):
    received = []
    for hop in (2, 1, 3):
        pairs = [(at, shift(at, hop)) for at in range(32)]
        part = lax.dynamic_index_in_dim(parts, (place + hop) % 4, 0, False)
        received.append(lax.ppermute(part, "dp", pairs))
    return lax.dynamic_index_in_dim(parts, place, 0, False) + received[0] + received[1] + received[2]


def add_x(total):
    along = lax.axis_index("dp") // 8
    total = total.reshape(4, 4, *total.shape[1:])
    return add_stage(total, along, lambda at, hop: (at // 8 + hop) % 4 * 8 + at % 8)


def add_z(total):
    along = (lax.axis_index("dp") // 2) % 4
    return add_stage(total, along, lambda at, hop: at // 8 * 8 + (at // 2 + hop) % 4 * 2 + at % 2)


def per_device(states, weights, bias, guesses, coarse_gain):
    section = lax.axis_index("layer")
    sections = lax.axis_size("layer")
    images = states.shape[1]
    scale = STEP / (images * lax.axis_size("dp"))
    paired = (images, PAIRS, 2, SIDE, CH)
    states = states.reshape(DEPTH, *paired)
    guess = guesses.reshape(paired)
    sent, slope, turned = run_first(states, weights, bias, guess, coarse_gain)

    parts = lax.all_to_all(sent.reshape(sections, -1, CH), "layer", 0, 0)
    begun = run_middle(parts, coarse_gain)
    begun = lax.all_to_all(begun, "layer", 0, 0).reshape(paired)

    adjoint, mine, other = run_upper(states, guess, begun, slope, turned, scale)
    upper = add_x(add_cores(mine, other))
    lower = add_x(add_cores(*run_lower(states, adjoint, slope, scale)))
    start = run_start(adjoint, slope, turned, guess.shape)
    total = add_z(jnp.concatenate([lower, upper], axis=1))
    bias_grad = lax.dynamic_slice_in_dim(total[:, ROWS, :], lax.axis_index("dp") * 4, 4, 1)
    return start.reshape(guesses.shape), total[:, :ROWS, :], bias_grad


def solution(mesh):
    return jax.shard_map(
        per_device,
        mesh=mesh,
        in_specs=(
            P("layer", "dp", None, None, None),
            P("layer", None, None),
            P("layer", None),
            P("layer", "dp", None, None, None),
            P(),
        ),
        out_specs=(P("layer", "dp", None, None, None), P("layer", "dp", None), P("layer", "dp")),
        check_vma=False,
    )
```

```python
import functools

import jax
import jax.numpy as jnp
from jax import lax
from jax.experimental import pallas as pl
from jax.experimental.pallas import tpu as pltpu
from jax.sharding import PartitionSpec as P


CH = 128
SIDE = 32
PAIRS = SIDE // 2
DEPTH = 3
TAPS = 9 * CH
TRIPLE = 3 * CH
STEP = 0.5
BLOCK = PAIRS
FINE = 4
ROWS = 36
SLAB = 40
EXCHANGE = ((2, 1), (2, 0), (0, 1), (1, 1), (3, 1), (1, 0), (3, 0))
TURNS = len(EXCHANGE)
f32 = jnp.float32
bf16 = jnp.bfloat16


def dot(a, b):
    return jnp.dot(a, b, preferred_element_type=f32)


def for_steps(images, body):
    steps = PAIRS // FINE

    def one(at, carry):
        body(at // steps, (at % steps) * FINE)
        return carry

    lax.fori_loop(0, images * steps, one, 0)


def clear_edges(ref):
    images = ref.shape[0]
    zero = jnp.zeros((images, 1, SIDE, TRIPLE), bf16)
    ref[:, 0:1, :, 0:TRIPLE] = zero
    ref[:, PAIRS : PAIRS + 1, :, TRIPLE:] = zero


def spread(ref, image, pair, half, value):
    rows = value.shape[0]
    column = lax.broadcasted_iota(jnp.int32, value.shape, 0) & (SIDE - 1)
    left = jnp.where(column == 0, 0.0, pltpu.roll(value, 1, 0))
    right = jnp.where(column == SIDE - 1, 0.0, pltpu.roll(value, rows - 1, 0))
    base = (1 - half) * TRIPLE
    for at, part in enumerate((left, value, right)):
        lanes = slice(base + at * CH, base + (at + 1) * CH)
        ref[image, pl.ds(pair + half, rows // SIDE), :, lanes] = part.astype(bf16).reshape(-1, SIDE, CH)


def convolve(ref, image, pair, kernel):
    upper = ref[image, pl.ds(pair, BLOCK)].reshape(BLOCK * SIDE, 2 * TRIPLE)
    lower = ref[image, pl.ds(pair + 1, BLOCK)].reshape(BLOCK * SIDE, 2 * TRIPLE)
    top, middle, bottom = (kernel[at * TRIPLE : (at + 1) * TRIPLE, :] for at in range(3))
    zero = jnp.zeros((TRIPLE, CH), bf16)

    def beside(left, right):
        return jnp.concatenate([jnp.concatenate(left, axis=0), jnp.concatenate(right, axis=0)], axis=1)

    return dot(upper, beside((top, middle), (zero, top))) + dot(lower, beside((bottom, zero), (middle, bottom)))


def gather(states, field, layer, image, pair, count):
    for half in range(2):
        value = states[layer, image, pl.ds(pair, count), half].reshape(count * SIDE, CH)
        spread(field, image, pair, half, value.astype(f32))


def first_kernel(*refs):
    states_from, weights_from, bias, guess_from, gain, slope_to, turned_to, own, *refs = refs
    leaving, refs = refs[:TURNS], refs[TURNS:]
    states, weights, guess, slope, turned, field, patches, adjoint, came, left = refs
    images = guess.shape[0]
    arrivals = {}
    for layer in reversed(range(DEPTH)):
        arrivals[layer] = [
            pltpu.make_async_copy(states_from.at[layer], states.at[layer], came.at[layer]),
            pltpu.make_async_copy(weights_from.at[layer], weights.at[layer], came.at[DEPTH + layer]),
        ]
        for copy in arrivals[layer]:
            copy.start()
        if layer == DEPTH - 1:
            guess_copy = pltpu.make_async_copy(guess_from, guess, came.at[2 * DEPTH])
            guess_copy.start()
    departures = []
    clear_edges(field)
    clear_edges(patches)
    section, sections = lax.axis_index("layer"), lax.axis_size("layer")
    inside = (section > 0) & (section < sections - 1)
    before = jnp.where(inside, gain[pl.ds(jnp.maximum(section - 1, 0), 1), :], 0.0).reshape(1, 1, CH)
    for layer in reversed(range(DEPTH)):
        last = layer == DEPTH - 1
        if last:
            for copy in arrivals[layer]:
                copy.wait()
            for_steps(images, lambda image, pair: gather(states, field, layer, image, pair, FINE))
        for tap in range(9):
            source = (8 - tap) * CH
            turned[layer, tap * CH : (tap + 1) * CH, :] = weights[layer, source : source + CH, :].T
        copy = pltpu.make_async_copy(turned.at[layer], turned_to.at[layer], left.at[DEPTH + layer])
        copy.start()
        departures.append(copy)
        if last:
            guess_copy.wait()
        offset = bias[layer : layer + 1, :]
        for image in range(images):
            both = convolve(field, image, 0, weights.at[layer])
            for half in range(2):
                lanes = slice(half * CH, (half + 1) * CH)
                value = jnp.tanh(both[:, lanes] + offset)
                value = 1.0 - value * value
                slope[layer, image, :, :, lanes] = value.reshape(PAIRS, SIDE, CH)
                now = guess[image, :, half] if last else adjoint[image, :, :, lanes]
                spread(patches, image, 0, half, value * now.reshape(PAIRS * SIDE, CH))
        copy = pltpu.make_async_copy(slope.at[layer], slope_to.at[layer], left.at[layer])
        copy.start()
        departures.append(copy)
        if layer:
            for copy in arrivals[layer - 1]:
                copy.wait()
        for image in range(images):
            both = convolve(patches, image, 0, turned.at[layer])
            for half in range(2):
                lanes = slice(half * CH, (half + 1) * CH)
                change = STEP * both[:, lanes].reshape(PAIRS, SIDE, CH)
                now = guess[image, :, half] if last else adjoint[image, :, :, lanes]
                if not layer:
                    now = now - before * guess[image, :, half]
                adjoint[image, :, :, lanes] = now + change
            if layer:
                gather(states, field, layer - 1, image, 0, PAIRS)
    per = PAIRS // FINE

    def piece(at):
        image, pair = at // per, at % per * FINE
        both = [adjoint[image, pl.ds(pair, FINE), :, half * CH : (half + 1) * CH] for half in range(2)]
        return jnp.stack(both, axis=1)

    own[...] = piece(section)
    for key, to in zip(EXCHANGE, leaving):
        to[...] = piece(receiver(section, sections, key))
    for copy in departures:
        copy.wait()


def start_copies(pairs, semaphores):
    copies = [pltpu.make_async_copy(source, to, semaphores.at[at]) for at, (source, to) in enumerate(pairs)]
    for copy in copies:
        copy.start()
    return copies


def scaled_rows(slope, now, patches, sums, image, pair):
    for half in range(2):
        lanes = slice(half * CH, (half + 1) * CH)
        value = slope[image, pl.ds(pair, FINE), :, lanes] * now(image, pair, half)
        value = value.reshape(FINE * SIDE, CH).astype(bf16).astype(f32)
        if sums is not None:
            sums[...] += value.reshape(-1, 8, CH).sum(axis=0)
        spread(patches, image, pair, half, value)


def weight_products(states, patches, grads, scale, beside=()):
    images = states.shape[0]
    points = images * PAIRS * SIDE
    halves = [states[:, :, half].reshape(points, CH) for half in range(2)]
    field = jnp.concatenate(halves, axis=1)
    beside = list(beside)
    share = -(-len(beside) // 6)
    for group in range(2):
        for third in range(3):
            lanes = slice(third * 2 * CH, (third + 1) * 2 * CH)
            part = patches[:, group : group + PAIRS, :, lanes].reshape(points, 2 * CH)
            only = {(0, 0): 0, (1, 2): 1}.get((group, third))
            left = field if only is None else halves[only]
            result = lax.dot_general(left, part, (((0,), (0,)), ((), ())), preferred_element_type=f32)
            for piece in range(2):
                row, side = divmod(third * 2 + piece, 3)
                for half in range(2) if only is None else (only,):
                    tap = row + 2 * group - half
                    if not 0 <= tap <= 2:
                        continue
                    block = ((2 - tap) * 3 + 2 - side) * CH
                    top = half * CH if only is None else 0
                    value = result[top : top + CH, piece * CH : (piece + 1) * CH] * scale
                    if (group, row, half) in ((0, 0, 0), (0, 1, 0), (1, 0, 0)):
                        grads[block : block + CH, :] = value
                    else:
                        grads[block : block + CH, :] += value
            for step in beside[:share]:
                step()
            beside = beside[share:]


def fill_slabs(grads, sums, scale, at, mine, other):
    core = lax.axis_index("dp") % 2
    total = scale * jnp.sum(sums[...], axis=0, keepdims=True)
    tail = jnp.broadcast_to(total, (SLAB - ROWS, CH))
    for chip in range(16):
        even = jnp.concatenate([grads[chip * 72 : chip * 72 + 36, :], tail], axis=0)
        odd = jnp.concatenate([grads[chip * 72 + 36 : chip * 72 + 72, :], tail], axis=0)
        mine[chip, at] = jnp.where(core == 0, even, odd)
        other[chip, at] = jnp.where(core == 0, odd, even)


def upper_kernel(scale, *refs):
    pieces, refs = refs[: TURNS + 1], refs[TURNS + 1 :]
    states_from, guess_from, slope_from, turned_from, adjoint_to, mine, other, *refs = refs
    states, guess, slope, turned, patches, adjoint, grads, sums, begun, came, left = refs
    images = guess.shape[0]
    (guess_copy,) = start_copies([(guess_from, guess)], came.at[0])
    arrivals = {
        layer: start_copies(
            [
                (slope_from.at[layer], slope.at[layer - 1]),
                (turned_from.at[layer], turned.at[layer - 1]),
                (states_from.at[layer], states.at[layer - 1]),
            ],
            came.at[layer],
        )
        for layer in (2, 1)
    }
    for at in range(2):
        clear_edges(patches.at[at])
    last = lax.axis_index("layer") == lax.axis_size("layer") - 1
    sums[...] = jnp.zeros_like(sums)
    begun[lax.axis_index("layer")] = pieces[0][...]
    for key, piece in zip(EXCHANGE, pieces[1:]):
        begun[sender(key)] = piece[...]

    def chosen(image, pair, half):
        there = begun[image * (PAIRS // FINE) + pair // FINE, :, half]
        now = jnp.where(last, guess[image, pl.ds(pair, FINE), half], there)
        adjoint[image, pl.ds(pair, FINE), :, half * CH : (half + 1) * CH] = now
        return now

    def held(image, pair, half):
        return adjoint[image, pl.ds(pair, FINE), :, half * CH : (half + 1) * CH]

    def back(at):
        for image in range(images):
            both = convolve(patches.at[at], image, 0, turned.at[at])
            for half in range(2):
                lanes = slice(half * CH, (half + 1) * CH)
                change = STEP * both[:, lanes].reshape(PAIRS, SIDE, CH)
                adjoint[image, :, :, lanes] = adjoint[image, :, :, lanes] + change

    guess_copy.wait()
    arrivals[2][0].wait()
    for_steps(images, lambda image, pair: scaled_rows(slope.at[1], chosen, patches.at[1], sums.at[1], image, pair))
    for copy in arrivals[2][1:] + arrivals[1]:
        copy.wait()
    back(1)
    steps = [
        functools.partial(scaled_rows, slope.at[0], held, patches.at[0], sums.at[0], image, pair)
        for image in range(images)
        for pair in range(0, PAIRS, FINE)
    ]
    weight_products(states.at[1], patches.at[1], grads.at[1], scale, steps)
    back(0)
    (away,) = start_copies([(adjoint, adjoint_to)], left)
    weight_products(states.at[0], patches.at[0], grads.at[0], scale)
    for at in range(2):
        fill_slabs(grads.at[at], sums.at[at], scale, at, mine, other)
    away.wait()


def lower_kernel(states_from, adjoint_from, slope_from, mine, other, states, adjoint, slope, patches, grads, sums, came, scale):
    images = adjoint.shape[0]
    copies = start_copies(
        [(slope_from.at[0], slope), (adjoint_from, adjoint), (states_from.at[0], states)], came
    )
    clear_edges(patches)
    sums[...] = jnp.zeros_like(sums)
    for copy in copies:
        copy.wait()

    def held(image, pair, half):
        return adjoint[image, pl.ds(pair, FINE), :, half * CH : (half + 1) * CH]

    for_steps(images, lambda image, pair: scaled_rows(slope, held, patches, sums, image, pair))
    weight_products(states, patches, grads, scale)
    fill_slabs(grads, sums, scale, 0, mine, other)


def start_kernel(adjoint_from, slope_from, turned_from, start, adjoint, slope, turned, patches, came):
    images = adjoint.shape[0]
    copies = start_copies(
        [(slope_from.at[0], slope), (adjoint_from, adjoint), (turned_from.at[0], turned)], came
    )
    clear_edges(patches)
    for copy in copies:
        copy.wait()

    def held(image, pair, half):
        return adjoint[image, pl.ds(pair, FINE), :, half * CH : (half + 1) * CH]

    for_steps(images, lambda image, pair: scaled_rows(slope, held, patches, None, image, pair))
    for image in range(images):
        both = convolve(patches, image, 0, turned)
        for half in range(2):
            lanes = slice(half * CH, (half + 1) * CH)
            change = STEP * both[:, lanes].reshape(PAIRS, SIDE, CH)
            start[image, :, half] = adjoint[image, :, :, lanes] + change


def sender(key):
    section, sections = lax.axis_index("layer"), lax.axis_size("layer")
    return (section // 2 + sections // 2 - key[0]) % (sections // 2) * 2 + (section + key[1]) % 2


def receiver(section, sections, key):
    return (section // 2 + key[0]) % (sections // 2) * 2 + (section + key[1]) % 2


def middle_kernel(*refs):
    own, gain, *refs = refs
    arrived, own_to, sent, parts, begun = refs[:TURNS], refs[TURNS], refs[TURNS + 1 : -2], refs[-2], refs[-1]
    section, count = lax.axis_index("layer"), parts.shape[0]
    parts[section] = own[...]
    for key, piece in zip(EXCHANGE, arrived):
        parts[sender(key)] = piece[...]
    carried = parts[count - 1]
    begun[count - 1] = carried
    begun[count - 2] = carried
    for at in range(count - 2, 0, -1):
        carried = parts[at] + gain[at - 1 : at, :].reshape(1, 1, 1, CH) * carried
        begun[at - 1] = carried
    own_to[...] = begun[section]
    for key, piece in zip(EXCHANGE, sent):
        piece[...] = begun[receiver(section, count, key)]


ANY = pl.BlockSpec(memory_space=pltpu.HBM)
VMEM = pl.BlockSpec(memory_space=pltpu.VMEM)


def limits(mib):
    return pltpu.CompilerParams(vmem_limit_bytes=mib * 1024 * 1024)


def run_first(states, weights, bias, guess, gain):
    images = guess.shape[0]
    pair_shape = (images, PAIRS, SIDE, 2 * CH)
    patch_shape = (images, PAIRS + 1, SIDE, 2 * TRIPLE)
    slope = (DEPTH, *pair_shape)
    return pl.pallas_call(
        first_kernel,
        out_shape=[jax.ShapeDtypeStruct(slope, f32), jax.ShapeDtypeStruct(weights.shape, bf16)]
        + [jax.ShapeDtypeStruct((FINE, 2, SIDE, CH), f32)] * (TURNS + 1),
        in_specs=[ANY, ANY, VMEM, ANY, VMEM],
        out_specs=[ANY, ANY] + [VMEM] * (TURNS + 1),
        scratch_shapes=[
            pltpu.VMEM(states.shape, bf16),
            pltpu.VMEM(weights.shape, bf16),
            pltpu.VMEM(guess.shape, f32),
            pltpu.VMEM(slope, f32),
            pltpu.VMEM(weights.shape, bf16),
            pltpu.VMEM(patch_shape, bf16),
            pltpu.VMEM(patch_shape, bf16),
            pltpu.VMEM(pair_shape, f32),
            pltpu.SemaphoreType.DMA((2 * DEPTH + 1,)),
            pltpu.SemaphoreType.DMA((2 * DEPTH,)),
        ],
        compiler_params=limits(60),
        name="first_relaxation",
    )(states, weights, bias, guess, gain)


def run_middle(own, gain, arrived):
    piece = jax.ShapeDtypeStruct(own.shape, f32)
    return pl.pallas_call(
        middle_kernel,
        out_shape=[piece] * (TURNS + 1),
        in_specs=[VMEM] * (TURNS + 2),
        out_specs=[VMEM] * (TURNS + 1),
        scratch_shapes=[pltpu.VMEM((TURNS + 1, *own.shape), f32)] * 2,
        compiler_params=limits(16),
        name="recurrence",
    )(own, gain, *arrived)


def cost(products, size):
    return pl.CostEstimate(flops=products * 4 * SIDE * SIDE * TAPS * CH, bytes_accessed=size, transcendentals=0)


def slabs(layers):
    return jax.ShapeDtypeStruct((16, layers, SLAB, CH), f32)


def run_upper(states, guess, pieces, slope, turned, scale):
    pair_shape, patch_shape = slope.shape[1:], (slope.shape[1], PAIRS + 1, SIDE, 2 * TRIPLE)
    return pl.pallas_call(
        functools.partial(upper_kernel, scale),
        out_shape=(jax.ShapeDtypeStruct(pair_shape, f32), slabs(2), slabs(2)),
        in_specs=[VMEM] * (TURNS + 1) + [ANY] * 4,
        out_specs=(ANY, VMEM, VMEM),
        scratch_shapes=[
            pltpu.VMEM((2, *states.shape[1:]), bf16),
            pltpu.VMEM(guess.shape, f32),
            pltpu.VMEM((2, *pair_shape), f32),
            pltpu.VMEM((2, *turned.shape[1:]), bf16),
            pltpu.VMEM((2, *patch_shape), bf16),
            pltpu.VMEM(pair_shape, f32),
            pltpu.VMEM((2, TAPS, CH), f32),
            pltpu.VMEM((2, 8, CH), f32),
            pltpu.VMEM((TURNS + 1, *pieces[0].shape), f32),
            pltpu.SemaphoreType.DMA((3, 3)),
            pltpu.SemaphoreType.DMA((1,)),
        ],
        compiler_params=limits(52),
        cost_estimate=cost(4, 8 << 20),
        name="upper_layers",
    )(*pieces, states, guess, slope, turned)


def run_lower(states, adjoint, slope, scale):
    patch_shape = (slope.shape[1], PAIRS + 1, SIDE, 2 * TRIPLE)
    return pl.pallas_call(
        functools.partial(lower_kernel, scale=scale),
        out_shape=(slabs(1), slabs(1)),
        in_specs=[ANY, ANY, ANY],
        out_specs=(VMEM, VMEM),
        scratch_shapes=[
            pltpu.VMEM(states.shape[1:], bf16),
            pltpu.VMEM(adjoint.shape, f32),
            pltpu.VMEM(slope.shape[1:], f32),
            pltpu.VMEM(patch_shape, bf16),
            pltpu.VMEM((TAPS, CH), f32),
            pltpu.VMEM((8, CH), f32),
            pltpu.SemaphoreType.DMA((3,)),
        ],
        compiler_params=limits(60),
        cost_estimate=cost(2, 4 << 20),
        name="lower_gradients",
    )(states, adjoint, slope)


def run_start(adjoint, slope, turned, shape):
    patch_shape = (slope.shape[1], PAIRS + 1, SIDE, 2 * TRIPLE)
    return pl.pallas_call(
        start_kernel,
        out_shape=jax.ShapeDtypeStruct(shape, f32),
        in_specs=[ANY, ANY, ANY],
        out_specs=VMEM,
        scratch_shapes=[
            pltpu.VMEM(adjoint.shape, f32),
            pltpu.VMEM(slope.shape[1:], f32),
            pltpu.VMEM(turned.shape[1:], bf16),
            pltpu.VMEM(patch_shape, bf16),
            pltpu.SemaphoreType.DMA((3,)),
        ],
        compiler_params=limits(60),
        cost_estimate=cost(1, 4 << 20),
        name="section_start",
    )(adjoint, slope, turned)


def add_cores(mine, other):
    return mine + lax.ppermute(other, "dp", [(at, at ^ 1) for at in range(32)])


def add_stage(parts, place, stride):
    received = []
    for hop in (2, 1, 3):
        pairs = [(at, at ^ (hop * stride)) for at in range(32)]
        part = lax.dynamic_index_in_dim(parts, place ^ hop, 0, False)
        received.append(lax.ppermute(part, "dp", pairs))
    return lax.dynamic_index_in_dim(parts, place, 0, False) + received[0] + received[1] + received[2]


def add_x(total):
    along = lax.axis_index("dp") // 8
    total = total.reshape(4, 4, *total.shape[1:])
    return add_stage(total, along, 8)


def add_z(total):
    along = (lax.axis_index("dp") // 2) % 4
    return add_stage(total, along, 2)


def per_device(states, weights, bias, guesses, coarse_gain):
    sections = lax.axis_size("layer")
    images = states.shape[1]
    scale = STEP / (images * lax.axis_size("dp"))
    paired = (images, PAIRS, 2, SIDE, CH)
    states = states.reshape(DEPTH, *paired)
    guess = guesses.reshape(paired)
    slope, turned, own, *leaving = run_first(states, weights, bias, guess, coarse_gain)

    def exchange(leaving):
        arrived = []
        for key, piece in zip(EXCHANGE, leaving):
            pairs = [(at, receiver(at, sections, key)) for at in range(sections)]
            arrived.append(lax.ppermute(piece, "layer", pairs))
        return arrived

    kept, *leaving = run_middle(own, coarse_gain, exchange(leaving))
    pieces = [kept] + exchange(leaving)

    adjoint, mine, other = run_upper(states, guess, pieces, slope, turned, scale)
    upper = add_x(add_cores(mine, other))
    lower = add_x(add_cores(*run_lower(states, adjoint, slope, scale)))
    start = run_start(adjoint, slope, turned, guess.shape)
    total = add_z(jnp.concatenate([lower, upper], axis=1))
    bias_grad = lax.dynamic_slice_in_dim(total[:, ROWS, :], lax.axis_index("dp") * 4, 4, 1)
    return start.reshape(guesses.shape), total[:, :ROWS, :], bias_grad


def solution(mesh):
    return jax.shard_map(
        per_device,
        mesh=mesh,
        in_specs=(
            P("layer", "dp", None, None, None),
            P("layer", None, None),
            P("layer", None),
            P("layer", "dp", None, None, None),
            P(),
        ),
        out_specs=(P("layer", "dp", None, None, None), P("layer", "dp", None), P("layer", "dp")),
        check_vma=False,
    )
```
